32 devices in a mesh: dp: 8 (over z, y), tensor: 4 (over x, core).
Axes of the slice: x: 2, y: 2, z: 4, core: 2. Of those that a mesh axis runs over, the one named last changes fastest.
Arguments:
- block_input: bfloat16 [8192, 1536], P(('dp', 'tensor')), may hold values from -6 to 6
- norm_gain: bfloat16 [1536], P('dp'), may hold values from 0.5 to 1.5
- gate_proj: bfloat16 [1536, 3072], P('dp', 'tensor'), may hold values from -0.15625 to 0.15625
- inner_proj: bfloat16 [1536, 3072], P('dp', 'tensor'), may hold values from -0.15625 to 0.15625
- step_proj: bfloat16 [1536, 48], P('dp', 'tensor'), may hold values from -0.15625 to 0.15625
- shared_proj: bfloat16 [1536, 256], P('dp'), may hold values from -0.15625 to 0.15625
- out_proj: bfloat16 [3072, 1536], P('tensor', 'dp'), may hold values from -0.109375 to 0.109375
- channel_params: bfloat16 [6, 48, 64], P(None, 'tensor', 'dp'), may hold values from -1 to 1.5, as said below
- shared_params: bfloat16 [5, 256], P(None, 'dp'), may hold values from -3 to 3
- head_params: float32 [3, 48], P(None, 'tensor'), may hold values from -7 to 3
- out_grad: bfloat16 [8192, 1536], P(('dp', 'tensor')), may hold values from -6 to 6
Outputs:
- block_output: bfloat16 [8192, 1536], P(('dp', 'tensor'))
- input_grad: float32 [8192, 1536], P(('dp', 'tensor'))
- norm_gain_grad: float32 [1536], P('dp')
- gate_proj_grad: float32 [1536, 3072], P('dp', 'tensor')
- inner_proj_grad: float32 [1536, 3072], P('dp', 'tensor')
- step_proj_grad: float32 [1536, 48], P('dp', 'tensor')
- shared_proj_grad: float32 [1536, 256], P('dp')
- out_proj_grad: float32 [3072, 1536], P('tensor', 'dp')
- channel_params_grad: float32 [6, 48, 64], P(None, 'tensor', 'dp')
- shared_params_grad: float32 [5, 256], P(None, 'dp')
- head_params_grad: float32 [3, 48], P(None, 'tensor')
The draws below stay inside these ranges and needn't reach their ends.
Inputs may be any that keep to these rules, and one draw needn't show every extreme that they name: `channel_params`: taps lie in -0.6 to 0.6, biases in -1 to 1, gains in 0.5 to 1.5.
All inputs are finite; a program needn't handle non-finite values.
Results may differ from the reference program's by a relative error of at most 0.02.
Values may be sent and summed in bfloat16 or wider, within the bound.
No kernel may reach another device: no remote copies, remote signals or barrier semaphores. Data moves between devices by JAX's collectives and lax.ppermute only.
A program may use at most 192 MiB of HBM per device.

```python
import math
import jax
import jax.numpy as jnp
from jax import lax

D = 1536
H = 48
P_SIZE = 64
N = 128
K = 4
CH = 256
SEQ_LEN = 1024
DI = 3072
TOKENS = 8192
N_DP = 8


def draw_channel_params(key, part):
    key_kernel, key_offset, key_scale = jax.random.split(jax.random.fold_in(key, 11), 3)
    kernel_rows = jax.random.uniform(key_kernel, (K, H, P_SIZE), jnp.float32, -0.6, 0.6)
    offset_row = jax.random.uniform(key_offset, (1, H, P_SIZE), jnp.float32, -1.0, 1.0)
    scale_row = jax.random.uniform(key_scale, (1, H, P_SIZE), jnp.float32, 0.5, 1.5)
    return jnp.concatenate([kernel_rows, offset_row, scale_row], axis=0).astype(jnp.bfloat16)


def draw_head_params(key, part):
    key_step, key_decay, key_skip = jax.random.split(jax.random.fold_in(key, 23), 3)
    step_target = jnp.exp(jax.random.uniform(key_step, (H,), jnp.float32, math.log(0.002), math.log(0.2)))
    step_offset = step_target + jnp.log(-jnp.expm1(-step_target))
    decay_log = jnp.log(jax.random.uniform(key_decay, (H,), jnp.float32, 1.0, 16.0))
    skip_scale = jax.random.uniform(key_skip, (H,), jnp.float32, 0.5, 1.5)
    return jnp.stack([step_offset, decay_log, skip_scale], axis=0)


def with_spikes(drawn, stream_key, source, target, shards_of, factor):
    owner, partner = [(jnp.arange(drawn.shape[axis_at]) // (drawn.shape[axis_at] // shards_of)).reshape([-1 if axis == axis_at else 1 for axis in range(drawn.ndim)]) for axis_at in (source, target)]
    chosen = jax.random.permutation(stream_key, shards_of)[partner]
    strong = (owner == chosen) | (owner == (partner + shards_of // 2) % shards_of)
    return jnp.where(strong, factor * drawn, drawn)


def steps_of(key, dims, shards, smallest, high):
    def one(position, shards_of):
        draws = jax.random.uniform(jax.random.fold_in(jax.random.fold_in(key, 6), position), (shards_of,), jnp.float32, smallest / len(shards), high / len(shards))
        return jnp.repeat(jnp.exp(draws), dims[position] // shards_of).reshape((-1,) + (1,) * (len(dims) - position - 1))

    gain = one(*shards[0])
    for cut in shards[1:]:
        gain = gain * one(*cut)
    return gain


def gaussian(rng, dims, width, bound, shards=(), dtype=jnp.bfloat16):
    array = jax.random.normal(rng, dims, jnp.float32) * width
    if len(shards) > 0:
        array = steps_of(rng, dims, shards, -0.22, 0.18) * array
    return jnp.clip(array, min=-bound, max=bound).astype(dtype)


def noise_with(own_key, dims, scale, reach, cuts, heavy, kind=jnp.bfloat16):
    result = scale * jax.random.normal(own_key, dims, jnp.float32)
    if cuts:
        result = result * steps_of(own_key, dims, cuts, -0.22, 0.18)
    return jnp.clip(with_spikes(result, jax.random.fold_in(own_key, 3), *heavy), -reach, reach).astype(kind)


def setup_inputs(seed: int = 0) -> dict:
    key_of = jax.random.split(jax.random.key(seed), 12)
    return {
        "block_input": gaussian(key_of[0], (TOKENS, D), 1.0, 6.0, ((0, 32),)),
        "norm_gain": jnp.clip(1.0 + 0.1 * jax.random.normal(key_of[1], (D,), jnp.float32), 0.5, 1.5).astype(jnp.bfloat16),
        "gate_proj": gaussian(key_of[2], (D, DI), D ** -0.5, 0.15625, ((0, 8), (1, 4))),
        "inner_proj": gaussian(key_of[3], (D, DI), D ** -0.5, 0.15625, ((0, 8), (1, 4))),
        "step_proj": gaussian(key_of[4], (D, H), D ** -0.5, 0.15625, ((0, 8), (1, 4))),
        "shared_proj": gaussian(key_of[5], (D, 2 * N), D ** -0.5, 0.15625, ((0, 8),)),
        "out_proj": gaussian(key_of[6], (DI, D), DI ** -0.5, 0.109375, ((0, 4), (1, 8))),
        "channel_params": draw_channel_params(jax.random.fold_in(key_of[11], 71), 0),
        "shared_params": gaussian(key_of[8], (K + 1, 2 * N), 0.5, 3.0, ((1, 8),)),
        "head_params": draw_head_params(jax.random.fold_in(key_of[11], 71), 0),
        "out_grad": noise_with(key_of[10], (TOKENS, D), 1.0, 6.0, ((0, 32),), (0, 1, 32, 2.75)),
    }


EPSILON = 1e-05
PRECISE = lax.Precision.HIGHEST

def rms_norm(token_rows, norm_scale):
    mean_square = lax.optimization_barrier(jnp.mean(token_rows * token_rows, axis=-1, keepdims=True))
    return token_rows * lax.rsqrt(mean_square + EPSILON) * norm_scale

def causal_conv(signal, kernel, offset_bias):
    kernel_size = kernel.shape[0]
    length = signal.shape[0]
    padded = jnp.pad(signal, ((kernel_size - 1, 0), (0, 0)))
    summed = jnp.zeros_like(signal) + offset_bias[None, :]
    for offset in range(kernel_size):
        summed = summed + kernel[offset][None, :] * padded[offset:offset + length]
    return summed

def ssd_scan(inner, step_size, decay_rate, in_state, out_state, block_len):
    length, heads, head_dim = inner.shape
    blocks = length // block_len
    states = in_state.shape[1]
    log_decay = -(step_size * decay_rate[None, :])
    cumulative = jnp.cumsum(log_decay.reshape(blocks, block_len, heads), axis=1)
    inner_blocks = inner.reshape(blocks, block_len, heads, head_dim)
    step_blocks = step_size.reshape(blocks, block_len, heads)
    in_blocks = in_state.reshape(blocks, block_len, states)
    out_blocks = out_state.reshape(blocks, block_len, states)
    weighted = inner_blocks * step_blocks[..., None]
    affinity = jnp.einsum('ctn,csn->cts', out_blocks, in_blocks, precision=PRECISE)
    lower = jnp.arange(block_len)[:, None] >= jnp.arange(block_len)[None, :]
    differ = cumulative[:, :, None, :] - cumulative[:, None, :, :]
    segment = jnp.exp(jnp.where(lower[None, :, :, None], differ, -jnp.inf))
    mixed = affinity[..., None] * segment
    intra = jnp.einsum('ctsh,cshp->cthp', mixed, weighted, precision=PRECISE)
    to_end = jnp.exp(cumulative[:, -1:, :] - cumulative)
    scaled_in = weighted * to_end[..., None]
    block_states = jnp.einsum('csn,cshp->chnp', in_blocks, scaled_in, precision=PRECISE)
    block_decay = jnp.exp(cumulative[:, -1, :])

    def advance(carry, pieces):
        state_piece, decay_piece = pieces
        return (decay_piece[:, None, None] * carry + state_piece, carry)
    start = jnp.zeros((heads, states, head_dim), jnp.float32)
    _, entering = lax.scan(advance, start, (block_states, block_decay))
    inter = jnp.einsum('ctn,chnp->cthp', out_blocks, entering, precision=PRECISE)
    inter = inter * jnp.exp(cumulative)[..., None]
    return (intra + inter).reshape(length, heads, head_dim)

def mixer(inner_raw, shared_raw, step_raw, gate_raw, channel_float, shared_float, head_params):
    kernel_size = shared_float.shape[0] - 1
    heads = head_params.shape[1]
    length = inner_raw.shape[0]
    flat_params = channel_float.reshape(channel_float.shape[0], -1)
    inner_act = jax.nn.silu(causal_conv(inner_raw, flat_params[:kernel_size], flat_params[kernel_size]))
    shared_act = jax.nn.silu(causal_conv(shared_raw, shared_float[:kernel_size], shared_float[kernel_size]))
    states = shared_act.shape[1] // 2
    step_size = jax.nn.softplus(step_raw + head_params[0][None, :])
    decay_rate = jnp.exp(head_params[1])
    inner_heads = inner_act.reshape(length, heads, -1)
    scanned = ssd_scan(inner_heads, step_size, decay_rate, shared_act[:, :states], shared_act[:, states:], CH)
    scanned = scanned + head_params[2][None, :, None] * inner_heads
    return scanned.reshape(length, -1) * jax.nn.silu(gate_raw)

def dot32(left, right):
    return jnp.dot(left, right, preferred_element_type=jnp.float32)

def reference(block_input, norm_gain, gate_proj, inner_proj, step_proj, shared_proj, out_proj, channel_params, shared_params, head_params, out_grad):
    tokens_seq = block_input.reshape(N_DP, SEQ_LEN, D)
    grads_seq = out_grad.reshape(N_DP, SEQ_LEN, D)
    gain_float = norm_gain.astype(jnp.float32)
    channel_float = channel_params.astype(jnp.float32)
    shared_float = shared_params.astype(jnp.float32)
    channel_gain = channel_float.reshape(K + 2, -1)[K + 1]

    def one_sequence(carry, pieces):
        seq_tokens, seq_grad = pieces
        residual_in = seq_tokens.astype(jnp.float32)
        normed, input_back = jax.vjp(rms_norm, residual_in, gain_float)
        normed_bf = normed.astype(jnp.bfloat16)
        gate_raw = dot32(normed_bf, gate_proj)
        inner_raw = dot32(normed_bf, inner_proj)
        shared_raw = dot32(normed_bf, shared_proj)
        step_raw = dot32(normed_bf, step_proj)
        gated, mixer_back = jax.vjp(mixer, inner_raw, shared_raw, step_raw, gate_raw, channel_float, shared_float, head_params)
        scaled, gate_back = jax.vjp(rms_norm, gated, channel_gain)
        scaled_bf = scaled.astype(jnp.bfloat16)
        branch = dot32(scaled_bf, out_proj)
        block_out = (residual_in + branch).astype(jnp.bfloat16)
        d_scaled = dot32(seq_grad, out_proj.T)
        d_out_proj = dot32(scaled_bf.T, seq_grad)
        d_gated, d_channel_gain = gate_back(d_scaled)
        d_inner, d_shared, d_step, d_gate, d_channel, d_shared_params, d_head = mixer_back(d_gated)
        d_channel = d_channel.reshape(K + 2, -1).at[K + 1].add(d_channel_gain).reshape(channel_float.shape)
        gate_bf = d_gate.astype(jnp.bfloat16)
        inner_bf = d_inner.astype(jnp.bfloat16)
        shared_bf = d_shared.astype(jnp.bfloat16)
        step_bf = d_step.astype(jnp.bfloat16)
        d_normed = dot32(gate_bf, gate_proj.T) + dot32(inner_bf, inner_proj.T)
        d_normed = d_normed + dot32(shared_bf, shared_proj.T) + dot32(step_bf, step_proj.T)
        d_residual, d_norm_gain = input_back(d_normed)
        input_grad = seq_grad.astype(jnp.float32) + d_residual
        terms = (d_norm_gain, dot32(normed_bf.T, gate_bf), dot32(normed_bf.T, inner_bf), dot32(normed_bf.T, step_bf), dot32(normed_bf.T, shared_bf), d_out_proj, d_channel, d_shared_params, d_head)
        new_carry = tuple((old + new for old, new in zip(carry, terms)))
        return (new_carry, (block_out, input_grad))
    start = (jnp.zeros((D,), jnp.float32), jnp.zeros((D, DI), jnp.float32), jnp.zeros((D, DI), jnp.float32), jnp.zeros((D, H), jnp.float32), jnp.zeros((D, 2 * N), jnp.float32), jnp.zeros((DI, D), jnp.float32), jnp.zeros((K + 2, H, P_SIZE), jnp.float32), jnp.zeros((K + 1, 2 * N), jnp.float32), jnp.zeros((3, H), jnp.float32))
    sums, stacked = lax.scan(one_sequence, start, (tokens_seq, grads_seq))
    block_output = stacked[0].reshape(TOKENS, D)
    input_grad = stacked[1].reshape(TOKENS, D)
    return (block_output, input_grad, sums[0], sums[1], sums[2], sums[3], sums[4], sums[5], sums[6], sums[7], sums[8])
```

```python
import functools
import jax
import jax.numpy as jnp
from jax import lax
from jax.experimental import pallas as pl
from jax.experimental.pallas import tpu as pltpu
from jax.sharding import PartitionSpec as P

BLOCK = 128
LANES = 128
EXACT = lax.Precision.HIGHEST
F32 = jnp.float32
BF16 = jnp.bfloat16


def mm(a, b, ca=1, cb=0, precision=None):
    return lax.dot_general(
        a, b, (((ca,), (cb,)), ((), ())), precision=precision, preferred_element_type=F32
    )


def sigmoid(v):
    return 0.5 * jnp.tanh(0.5 * v) + 0.5


def softplus(v):
    return jnp.maximum(v, 0.0) + jnp.log1p(jnp.exp(-jnp.abs(v)))


def earlier(cur, prev, k):
    if k == 0:
        return cur
    return jnp.concatenate([prev[8 - k :], cur[: cur.shape[0] - k]], axis=0)


def later(cur, after, k):
    if k == 0:
        return cur
    return jnp.concatenate([cur[k:], after[:k]], axis=0)


def iota2(axis):
    return lax.broadcasted_iota(jnp.int32, (BLOCK, LANES), axis)


def column(array, h):
    return jnp.broadcast_to(array[:, h : h + 1], (BLOCK, LANES))


def forward_kernel(
    taps, inner_ref, side_ref, chan_ref, shp_ref, head_ref,
    scan_ref, state_ref, bc_ref, step_ref, cum_ref, carry, tail, side_tail,
):
    @pl.when(pl.program_id(0) == 0)
    def _():
        carry[...] = jnp.zeros_like(carry)
        tail[...] = jnp.zeros_like(tail)
        side_tail[...] = jnp.zeros_like(side_tail)

    rows, lanes = iota2(0), iota2(1)
    low = lanes < LANES // 2
    causal = rows >= lanes
    shared = side_ref[:, : 2 * LANES]
    conv = shp_ref[taps : taps + 1]
    for k in range(taps):
        conv = conv + shp_ref[k : k + 1] * earlier(shared, side_tail[...], taps - 1 - k)
    side_tail[...] = shared[BLOCK - 8 :]
    bc = (conv * sigmoid(conv)).astype(BF16)
    bc_ref[...] = bc
    b_act, c_act = bc[:, :LANES], bc[:, LANES:]
    b_turned = b_act.T
    step = softplus(side_ref[:, 2 * LANES :] + head_ref[0:1])
    step_ref[...] = step
    cum = mm(causal.astype(F32), step * head_ref[1:2], precision=EXACT)
    cum_ref[...] = cum
    cum_turned = cum.T
    affinity = jnp.where(causal, mm(c_act, b_act, 1, 1), 0.0)
    for pair in range(inner_ref.shape[1] // LANES):
        at = slice(pair * LANES, (pair + 1) * LANES)
        raw, before = inner_ref[:, at], tail[:, at]
        conv = chan_ref[taps : taps + 1, at]
        for k in range(taps):
            conv = conv + chan_ref[k : k + 1, at] * earlier(raw, before, taps - 1 - k)
        tail[:, at] = raw[BLOCK - 8 :]
        act = conv * sigmoid(conv)
        cums = [column(cum, 2 * pair + i) for i in range(2)]
        cum_wide = jnp.where(low, cums[0], cums[1])
        step_wide = jnp.where(low, column(step, 2 * pair), column(step, 2 * pair + 1))
        last = cum_wide[BLOCK - 1 :]
        weighted = act * step_wide
        weighted_bf = weighted.astype(BF16)
        zero = jnp.zeros_like(weighted_bf)
        mixed = [
            (
                jnp.exp(jnp.minimum(cums[i] - cum_turned[2 * pair + i : 2 * pair + i + 1], 0.0))
                * affinity
            ).astype(BF16)
            for i in range(2)
        ]
        inside = mm(
            jnp.concatenate(mixed, axis=1),
            jnp.concatenate(
                [jnp.where(low, weighted_bf, zero), jnp.where(low, zero, weighted_bf)], axis=0
            ),
        )
        state = carry[:, at]
        state_bf = state.astype(BF16)
        state_ref[0, :, at] = state_bf
        across = mm(c_act, state_bf) * jnp.exp(cum_wide)
        scan_ref[:, at] = inside + across + chan_ref[taps + 2 : taps + 3, at] * act
        fed = (weighted * jnp.exp(last - cum_wide)).astype(BF16)
        carry[:, at] = jnp.exp(last) * state + mm(b_turned, fed)


def scan_forward(taps, inner_raw, side_raw, chan, shp, head):
    length, width = inner_raw.shape
    blocks = length // BLOCK
    row = lambda w: pl.BlockSpec((BLOCK, w), lambda i: (i, 0))
    whole = lambda a: pl.BlockSpec(a.shape, lambda i: (0,) * a.ndim)
    return pl.pallas_call(
        functools.partial(forward_kernel, taps),
        grid=(blocks,),
        in_specs=[row(width), row(3 * LANES), whole(chan), whole(shp), whole(head)],
        out_specs=[
            row(width),
            pl.BlockSpec((1, LANES, width), lambda i: (i, 0, 0)),
            row(2 * LANES),
            row(LANES),
            row(LANES),
        ],
        out_shape=[
            jax.ShapeDtypeStruct((length, width), F32),
            jax.ShapeDtypeStruct((blocks, LANES, width), BF16),
            jax.ShapeDtypeStruct((length, 2 * LANES), BF16),
            jax.ShapeDtypeStruct((length, LANES), F32),
            jax.ShapeDtypeStruct((length, LANES), F32),
        ],
        scratch_shapes=[
            pltpu.VMEM((LANES, width), F32),
            pltpu.VMEM((8, width), F32),
            pltpu.VMEM((8, 2 * LANES), F32),
        ],
        cost_estimate=pl.CostEstimate(
            flops=2 * length * width * 5 * LANES,
            transcendentals=length * width * 6,
            bytes_accessed=length * width * 12,
        ),
        name="scan_forward",
    )(inner_raw, side_raw, chan, shp, head)


def backward_kernel(
    taps, first_pair, final, inner_ref, before_ref, dscan_ref, bc_ref, step_ref, cum_ref, side_ref,
    side_before_ref, state_ref, chan_ref, shp_ref, head_ref, dbc_in_ref, dstep_in_ref,
    dinner_ref, dbc_ref, dstep_ref, dchan_ref, dhead_ref, dshp_ref,
    dstate, after, side_after,
):
    place = pl.num_programs(0) - 1 - pl.program_id(0)

    @pl.when(pl.program_id(0) == 0)
    def _():
        dstate[...] = jnp.zeros_like(dstate)
        after[...] = jnp.zeros_like(after)
        side_after[...] = jnp.zeros_like(side_after)
        dchan_ref[...] = jnp.zeros_like(dchan_ref)
        dhead_ref[...] = jnp.zeros_like(dhead_ref)
        dshp_ref[...] = jnp.zeros_like(dshp_ref)

    rows, lanes = iota2(0), iota2(1)
    low = lanes < LANES // 2
    causal = rows >= lanes
    inside_sequence = jnp.where(place > 0, 1.0, 0.0)
    bc = bc_ref[...]
    b_act, c_act = bc[:, :LANES], bc[:, LANES:]
    c_turned = c_act.T
    step, cum = step_ref[...], cum_ref[...]
    cum_turned = cum.T
    affinity = jnp.where(causal, mm(c_act, b_act, 1, 1), 0.0)
    d_affinity = jnp.zeros((BLOCK, LANES), F32)
    row_sums = jnp.zeros((BLOCK, LANES), F32)
    column_sums = jnp.zeros((16, LANES), F32)
    sub = lax.broadcasted_iota(jnp.int32, (16, LANES), 0)
    width = inner_ref.shape[1]
    summed = [[], [], [], [], []]
    dye_all, state_all, fed_all, dstate_all = [], [], [], []
    for pair in range(width // LANES):
        at = slice(pair * LANES, (pair + 1) * LANES)
        head = 2 * (first_pair + pair)
        raw, before = inner_ref[:, at], before_ref[:, at] * inside_sequence
        shifted = [earlier(raw, before, taps - 1 - k) for k in range(taps)]
        conv = chan_ref[taps : taps + 1, at]
        for k in range(taps):
            conv = conv + chan_ref[k : k + 1, at] * shifted[k]
        gate = sigmoid(conv)
        act = conv * gate
        slope = gate + act * (1.0 - gate)
        cums = [column(cum, head + i) for i in range(2)]
        cum_wide = jnp.where(low, cums[0], cums[1])
        step_wide = jnp.where(low, column(step, head), column(step, head + 1))
        last = cum_wide[BLOCK - 1 :]
        to_here, to_end, through = jnp.exp(cum_wide), jnp.exp(last - cum_wide), jnp.exp(last)
        weighted = act * step_wide
        weighted_bf = weighted.astype(BF16)
        dy = dscan_ref[:, at].astype(F32)
        dy_bf = dy.astype(BF16)
        zero = jnp.zeros_like(dy_bf)
        dy_split = jnp.concatenate([jnp.where(low, dy_bf, zero), jnp.where(low, zero, dy_bf)], axis=0)
        d_mixed = mm(dy_split, weighted_bf, 1, 1)
        mixed = []
        for i in range(2):
            decay = jnp.exp(jnp.minimum(cums[i] - cum_turned[head + i : head + i + 1], 0.0))
            grad = d_mixed[i * BLOCK : (i + 1) * BLOCK] * decay
            d_affinity = d_affinity + grad
            product = grad * affinity
            row_sums = row_sums + jnp.where(
                lanes == head + i, jnp.sum(product, axis=1, keepdims=True), 0.0
            )
            column_sums = column_sums + jnp.where(
                sub == head + i, jnp.sum(product, axis=0, keepdims=True), 0.0
            )
            mixed.append((decay * affinity).astype(BF16))
        d_inside = mm(jnp.concatenate(mixed, axis=0), dy_split, 0, 0)
        state_bf = state_ref[0, :, at]
        entered = mm(c_act, state_bf)
        dye = dy * to_here
        dye_bf = dye.astype(BF16)
        d_state = dstate[:, at]
        d_state_bf = d_state.astype(BF16)
        d_fed = to_end * mm(b_act, d_state_bf)
        d_weighted = d_inside + d_fed
        summed[0].append((dye * entered).astype(BF16))
        summed[1].append((weighted * d_fed).astype(BF16))
        summed[2].append((d_weighted * act).astype(BF16))
        summed[3].append((dy * act).astype(BF16))
        summed[4].append(
            jnp.broadcast_to(
                through * jnp.sum(d_state * state_bf.astype(F32), axis=0, keepdims=True), (16, LANES)
            ).astype(BF16)
        )
        dye_all.append(dye_bf)
        state_all.append(state_bf)
        fed_all.append((weighted * to_end).astype(BF16))
        dstate_all.append(d_state_bf)
        dstate[:, at] = through * d_state + mm(c_turned, dye_bf)
        d_act = step_wide * d_weighted + chan_ref[taps + 2 : taps + 3, at] * dy
        d_conv = d_act * slope
        d_raw = jnp.zeros_like(d_conv)
        for k in range(taps):
            d_raw = d_raw + chan_ref[k : k + 1, at] * later(d_conv, after[:, at], taps - 1 - k)
            dchan_ref[k : k + 1, at] += jnp.sum(d_conv * shifted[k], axis=0, keepdims=True)
        dchan_ref[taps : taps + 1, at] += jnp.sum(d_conv, axis=0, keepdims=True)
        after[:, at] = d_conv[:8]
        dinner_ref[:, at] = d_raw.astype(BF16)
    join = lambda parts: jnp.concatenate(parts, axis=1)
    where_row = lax.broadcasted_iota(jnp.int32, (width, LANES), 0)
    where_lane = lax.broadcasted_iota(jnp.int32, (width, LANES), 1)
    to_heads = jnp.where(where_row // (LANES // 2) + 2 * first_pair == where_lane, 1.0, 0.0).astype(BF16)
    totals = mm(jnp.concatenate([join(s) for s in summed], axis=0), to_heads)
    from_past, to_future, d_step_here, d_skip = [
        totals[i * BLOCK : (i + 1) * BLOCK] for i in range(4)
    ]
    carried = totals[4 * BLOCK : 4 * BLOCK + 1]
    column_sums = jnp.concatenate(
        [column_sums, jnp.zeros((BLOCK - 16, LANES), F32)], axis=0
    ).T
    d_cum = row_sums - column_sums + from_past
    d_log = (
        mm((lanes >= rows).astype(F32), d_cum, precision=EXACT)
        + mm((lanes < rows).astype(F32), to_future, precision=EXACT)
        + carried
    )
    decay_rate = head_ref[1:2]
    d_step = (d_log * decay_rate + d_step_here) * sigmoid(side_ref[:, 2 * LANES :] + head_ref[0:1])
    dstep_ref[...] = dstep_in_ref[...] + d_step
    for i, terms in enumerate((d_step, d_log * step * decay_rate, d_skip)):
        dhead_ref[i : i + 1] += jnp.sum(terms, axis=0, keepdims=True)
    d_affinity_bf = jnp.where(causal, d_affinity, 0.0).astype(BF16)
    d_b = mm(d_affinity_bf, c_act, 0, 0) + mm(join(fed_all), join(dstate_all), 1, 1)
    d_c = mm(d_affinity_bf, b_act) + mm(join(dye_all), join(state_all), 1, 1)
    dbc = dbc_in_ref[...] + join([d_b, d_c])
    if not final:
        dbc_ref[...] = dbc
    else:
        shared = side_ref[:, : 2 * LANES]
        before = side_before_ref[:, : 2 * LANES] * inside_sequence
        shifted = [earlier(shared, before, taps - 1 - k) for k in range(taps)]
        conv = shp_ref[taps : taps + 1]
        for k in range(taps):
            conv = conv + shp_ref[k : k + 1] * shifted[k]
        gate = sigmoid(conv)
        d_conv = dbc * (gate + conv * gate * (1.0 - gate))
        d_raw = jnp.zeros_like(d_conv)
        for k in range(taps):
            d_raw = d_raw + shp_ref[k : k + 1] * later(d_conv, side_after[...], taps - 1 - k)
            dshp_ref[k : k + 1] += jnp.sum(d_conv * shifted[k], axis=0, keepdims=True)
        dshp_ref[taps : taps + 1] += jnp.sum(d_conv, axis=0, keepdims=True)
        side_after[...] = d_conv[:8]
        dbc_ref[...] = d_raw.astype(dbc_ref.dtype)


def scan_backward(taps, group, groups, inner_raw, dscan, saved, side_raw, chan, shp, head, dbc, dstep):
    state, bc, step, cum = saved
    length = inner_raw.shape[0]
    width = inner_raw.shape[1] // groups
    blocks = length // BLOCK
    final = group == groups - 1
    turn = lambda i: blocks - 1 - i
    row = lambda w, g=0: pl.BlockSpec((BLOCK, w), lambda i: (turn(i), g))
    ahead = lambda w, g=0: pl.BlockSpec(
        (8, w), lambda i: (jnp.maximum(turn(i) * (BLOCK // 8) - 1, 0), g)
    )
    fixed = lambda h, w, g=0: pl.BlockSpec((h, w), lambda i: (0, g))
    return pl.pallas_call(
        functools.partial(backward_kernel, taps, group * (width // LANES), final),
        grid=(blocks,),
        in_specs=[
            row(width, group), ahead(width, group), row(width, group), row(2 * LANES), row(LANES),
            row(LANES), row(3 * LANES), ahead(3 * LANES),
            pl.BlockSpec((1, LANES, width), lambda i: (turn(i), 0, group)),
            fixed(chan.shape[0], width, group), fixed(*shp.shape), fixed(*head.shape),
            row(2 * LANES), row(LANES),
        ],
        out_specs=[
            row(width), row(2 * LANES), row(LANES), fixed(8, width), fixed(8, LANES),
            fixed(8, 2 * LANES),
        ],
        out_shape=[
            jax.ShapeDtypeStruct((length, width), BF16),
            jax.ShapeDtypeStruct((length, 2 * LANES), BF16 if final else F32),
            jax.ShapeDtypeStruct((length, LANES), F32),
            jax.ShapeDtypeStruct((8, width), F32),
            jax.ShapeDtypeStruct((8, LANES), F32),
            jax.ShapeDtypeStruct((8, 2 * LANES), F32),
        ],
        scratch_shapes=[
            pltpu.VMEM((LANES, width), F32),
            pltpu.VMEM((8, width), F32),
            pltpu.VMEM((8, 2 * LANES), F32),
        ],
        cost_estimate=pl.CostEstimate(
            flops=2 * length * width * 16 * LANES,
            transcendentals=length * width * 8,
            bytes_accessed=length * width * 16,
        ),
    )(
        inner_raw, inner_raw, dscan, bc, step, cum, side_raw, side_raw, state, chan, shp, head, dbc, dstep
    )


def digits(count):
    bits, sizes = count.bit_length() - 1, []
    while bits > 0:
        sizes.append(4 if bits > 1 else 2)
        bits -= 2 if bits > 1 else 1
    return sizes


def exchange(x, axis, distance):
    count = lax.axis_size(axis)
    return lax.ppermute(x, axis, [(i, i ^ distance) for i in range(count)])


def gather(x, axis, stacked=False):
    pieces = {0: x}
    stride = lax.axis_size(axis)
    for size in digits(stride) if axis == "dp" else (2, 2):
        stride //= size
        held = list(pieces.items())
        for k in range(1, size):
            if stacked and len(held) > 1:
                got = exchange(jnp.concatenate([p for _, p in held], axis=0), axis, k * stride)
                parts = jnp.split(got, len(held), axis=0)
            else:
                parts = []
                for key, piece in held:
                    parts.append(exchange(piece, axis, k * stride))
            for (key, _), part in zip(held, parts):
                pieces[key ^ (k * stride)] = part
    return pieces


def assemble(pieces, axis):
    me = lax.axis_index(axis)
    first = pieces[0]
    whole = jnp.zeros((first.shape[0] * len(pieces),) + first.shape[1:], first.dtype)
    for key, piece in pieces.items():
        start = (me ^ key) * first.shape[0]
        whole = lax.dynamic_update_slice(whole, piece, (start,) + (0,) * (first.ndim - 1))
    return whole


def reduce_scatter(x, axis):
    me = lax.axis_index(axis)
    stride = 1
    for size in reversed(digits(lax.axis_size(axis)) if axis == "dp" else (2, 2)):
        digit = (me // stride) % size
        x = x.reshape((x.shape[0] // size, size) + x.shape[1:])
        pick = lambda i: lax.dynamic_index_in_dim(x, i, 1, keepdims=False)
        total = pick(digit).astype(F32)
        for k in range(1, size):
            total = total + exchange(pick(digit ^ k).astype(BF16), axis, k * stride).astype(F32)
        x = total
        stride *= size
    return x[0]


def all_sum(x):
    for distance in (1, 2):
        x = x + exchange(x, "tensor", distance)
    return x


def pad_to(x, *shape):
    return jnp.pad(x, [(0, n - m) for n, m in zip(shape, x.shape)])


GROUPS = 3
EPSILON = 1e-05


def shards(
    block_input, norm_gain, gate_proj, inner_proj, step_proj, shared_proj, out_proj,
    channel_params, shared_params, head_params, out_grad,
):
    ranks, ways = lax.axis_size("dp"), lax.axis_size("tensor")
    here = lax.axis_index("tensor")
    tokens, model = block_input.shape[0] * ways, block_input.shape[1]
    rows, width = inner_proj.shape
    heads, states = head_params.shape[1], shared_proj.shape[1] // 2
    size = width // heads
    taps = shared_params.shape[0] - 1
    part = shared_proj.shape[1] // ways
    gain_rows = -(-rows // LANES)
    channel_rows = (taps + 2) * heads

    side_shard = pad_to(
        jnp.concatenate(
            [lax.dynamic_slice_in_dim(shared_proj, here * part, part, 1), step_proj], axis=1
        ),
        rows, LANES,
    )
    extra_shard = jnp.concatenate(
        [
            pad_to(channel_params.reshape(channel_rows, -1), channel_rows, LANES),
            pad_to(shared_params, 8, LANES),
            pad_to(pad_to(norm_gain, gain_rows * LANES).reshape(gain_rows, LANES), 16, LANES),
        ],
        axis=0,
    )
    side_pieces = gather(jnp.concatenate([side_shard, extra_shard], axis=0), "dp", True)
    input_full = assemble(gather(block_input, "tensor"), "tensor")
    inner_full = assemble(gather(inner_proj, "dp"), "dp")
    gate_full = assemble(gather(gate_proj, "dp"), "dp")
    out_full = assemble(gather(out_proj.T, "dp"), "dp")
    cot_full = assemble(gather(out_grad, "tensor"), "tensor")

    side_full = assemble({k: v[:rows] for k, v in side_pieces.items()}, "dp")
    extras = assemble({k: v[rows:][None] for k, v in side_pieces.items()}, "dp")
    spread = extras[:, :channel_rows, : size // ranks].reshape(ranks, taps + 2, heads, size // ranks)
    channel = spread.transpose(1, 2, 0, 3).reshape(taps + 2, width).astype(F32)
    shared_small = extras[:, channel_rows : channel_rows + taps + 1, : 2 * states // ranks]
    shared_small = shared_small.transpose(1, 0, 2).reshape(taps + 1, 2 * states).astype(F32)
    gain = extras[:, channel_rows + 8 : channel_rows + 8 + gain_rows]
    gain = gain.reshape(ranks, -1)[:, :rows].reshape(model).astype(F32)
    chan = jnp.concatenate(
        [channel, jnp.repeat(head_params[2], size)[None], jnp.zeros((1, width), F32)], axis=0
    )
    shp = pad_to(shared_small, 8, 2 * states)
    head = pad_to(jnp.stack([head_params[0], -jnp.exp(head_params[1])]), 8, LANES)

    quarters = {k: v[:, :part] for k, v in gather(side_full, "tensor").items()}
    for bit in (1, 2):
        swap = (here & bit) != 0
        quarters = {k: jnp.where(swap, quarters[k ^ bit], v) for k, v in quarters.items()}
    side_weight = jnp.concatenate(
        [quarters[k] for k in range(ways)] + [pad_to(side_full[:, part : part + heads], model, LANES)],
        axis=1,
    )

    input_float = input_full.astype(F32)
    inverse_in = lax.rsqrt(jnp.mean(input_float * input_float, axis=1, keepdims=True) + EPSILON)
    normed = (input_float * inverse_in * gain[None]).astype(BF16)
    inner_raw = mm(normed, inner_full)
    side_raw = mm(normed, side_weight)
    scanned, state, bc, step, cum = scan_forward(taps, inner_raw, side_raw, chan, shp, head)
    gate_raw = mm(normed, gate_full)
    gate_half = sigmoid(gate_raw)
    gate_act = gate_raw * gate_half
    gated = scanned * gate_act
    channels = width * ways
    channel_gain = channel[taps + 1][None]
    squares = all_sum(jnp.sum(gated * gated, axis=1))
    inverse_gate = lax.rsqrt(squares / channels + EPSILON)[:, None]
    scaled = (gated * inverse_gate * channel_gain).astype(BF16)
    d_out = mm(cot_full, scaled, 0, 0).astype(BF16)
    out_grad_w = reduce_scatter(d_out.reshape(ranks, rows, width), "dp").T
    d_scaled = mm(cot_full, out_full)
    weighted = d_scaled * channel_gain
    cross = all_sum(jnp.sum(weighted * gated, axis=1))[:, None]
    branch = mm(scaled, out_full, 1, 1).astype(BF16)
    branch = reduce_scatter(branch.reshape(ways, -1, model), "tensor")
    block_output = (block_input.astype(F32) + branch).astype(BF16)

    d_gated = inverse_gate * weighted - gated * (inverse_gate**3 * cross / channels)
    d_gain = jnp.sum(d_scaled * gated * inverse_gate, axis=0, keepdims=True)
    d_scanned = d_gated * gate_act
    d_gate = (d_gated * scanned * (gate_half + gate_act * (1.0 - gate_half))).astype(BF16)
    d_gate_w = mm(normed, d_gate, 0, 0).astype(BF16)
    gate_grad = reduce_scatter(d_gate_w.reshape(ranks, rows, width), "dp")
    dbc = jnp.zeros((tokens, 2 * states), F32)
    d_step = jnp.zeros((tokens, LANES), F32)
    d_head = jnp.zeros((8, LANES), F32)
    d_inner, d_chan, inner_grad = [], [], []
    for group in range(GROUPS):
        part_inner, dbc, d_step, part_chan, part_head, d_shp = scan_backward(
            taps, group, GROUPS, inner_raw, d_scanned, (state, bc, step, cum), side_raw, chan, shp,
            head, dbc, d_step,
        )
        d_inner.append(part_inner)
        d_chan.append(part_chan)
        d_head = d_head + part_head
        d_inner_w = mm(normed, part_inner, 0, 0).astype(BF16)
        inner_grad.append(reduce_scatter(d_inner_w.reshape(ranks, rows, -1), "dp"))
    inner_grad = jnp.concatenate(inner_grad, axis=1)
    d_side = jnp.concatenate([dbc, d_step.astype(BF16)], axis=1)
    d_normed = mm(d_gate, gate_full, 1, 1) + mm(jnp.concatenate(d_inner, axis=1), inner_full, 1, 1)
    d_normed = d_normed + mm(d_side, side_weight, 1, 1)
    own = reduce_scatter(d_normed.astype(BF16).reshape(ways, -1, model), "tensor")
    d_norm_gain = jnp.sum(d_normed * input_float * inverse_in, axis=0)

    d_shared_w = mm(normed, dbc, 0, 0)
    d_step_w = mm(d_step.astype(BF16), normed, 0, 0)[:heads]
    quarter_rows = rows // ways
    both = jnp.concatenate([d_norm_gain.reshape(-1, 2 * states), d_shp], axis=0)
    terms = d_shared_w.reshape(ranks, ways, quarter_rows, 2 * states).transpose(1, 0, 2, 3)
    terms = terms.reshape(ways, ranks * quarter_rows, 2 * states)
    terms = jnp.concatenate([terms, jnp.broadcast_to(both, (ways,) + both.shape)], axis=1)
    summed = reduce_scatter(terms, "tensor")
    d_shared_w = summed[: ranks * quarter_rows].reshape(ranks, quarter_rows, 2 * states)
    d_norm_gain = summed[ranks * quarter_rows : ranks * quarter_rows + model // (2 * states)]
    d_shp = summed[ranks * quarter_rows + model // (2 * states) :]
    by_rank = lambda x: x.reshape(x.shape[0], ranks, -1).transpose(1, 0, 2)
    d_channel = jnp.concatenate([jnp.concatenate(d_chan, axis=1)[: taps + 1], d_gain], axis=0)
    d_channel = d_channel.reshape(taps + 2, heads, ranks, -1).transpose(2, 0, 1, 3)
    wide = lambda x, n: jnp.pad(x, ((0, 0), (0, n - x.shape[1]), (0, 2 * states - x.shape[2])))
    small = jnp.concatenate(
        [
            d_shared_w,
            wide(by_rank(jnp.concatenate([d_step_w, d_norm_gain.reshape(1, model)], axis=0)), 16),
            wide(d_channel.reshape(ranks, taps + 2, -1), 8),
            wide(by_rank(d_shp[: taps + 1]), 8),
            wide(jnp.broadcast_to(d_head[:3, :heads], (ranks, 3, heads)), 8),
        ],
        axis=1,
    )
    small = reduce_scatter(small, "dp")
    shared_grad = assemble(gather(small[:quarter_rows], "tensor"), "tensor")
    at = quarter_rows
    step_grad = small[at : at + heads, :rows].T
    gain_grad = small[at + heads, :rows]
    channel_grad = small[at + 16 : at + 18 + taps, : heads * size // ranks]
    channel_grad = channel_grad.reshape(taps + 2, heads, size // ranks)
    shared_param_grad = small[at + 24 : at + 25 + taps, : 2 * states // ranks]
    head_grad = small[at + 32 : at + 35, :heads]

    residual = block_input.astype(F32)
    inverse = lax.rsqrt(jnp.mean(residual * residual, axis=1, keepdims=True) + EPSILON)
    weighted_in = own * gain[None]
    input_grad = (
        out_grad.astype(F32)
        + inverse * weighted_in
        - residual * (inverse**3 * jnp.mean(weighted_in * residual, axis=1, keepdims=True))
    )
    return (
        block_output, input_grad, gain_grad, gate_grad, inner_grad, step_grad, shared_grad,
        out_grad_w, channel_grad, shared_param_grad, head_grad,
    )


def solution(mesh):
    rows, weights = P(("dp", "tensor"), None), P("dp", "tensor")
    in_specs = (
        rows, P("dp"), weights, weights, weights, P("dp", None), P("tensor", "dp"),
        P(None, "tensor", "dp"), P(None, "dp"), P(None, "tensor"), rows,
    )
    out_specs = (rows,) + in_specs[:1] + in_specs[1:4] + in_specs[4:10]

    return jax.shard_map(shards, mesh=mesh, in_specs=in_specs, out_specs=out_specs, check_vma=False)
```
